32 devices in a mesh: dp: 4 (over y, core), seq: 8 (over z, x).
Axes of the slice: x: 2, y: 2, z: 4, core: 2. Of those that a mesh axis runs over, the one named last changes fastest.
Arguments:
- mixer_in: bfloat16 [4, 2048, 2560], P('dp', 'seq'), may hold values from -6 to 6
- step_raw: float32 [4, 40, 2048], P('dp', None, 'seq'), may hold values from -3 to 3
- key_proj: bfloat16 [4, 2048, 128], P('dp', 'seq'), may hold values from -0.3125 to 0.3125
- query_proj: bfloat16 [4, 2048, 128], P('dp', 'seq'), may hold values from -0.3125 to 0.3125
- codec_ids: int32 [4, 2048], P('dp', 'seq'), may hold values from 0 to 1023
- finger_ids: int32 [4, 2048], P('dp', 'seq'), may hold values from 0 to 4, as said below
- fret_ids: int32 [4, 2048], P('dp', 'seq'), may hold values from 0 to 24, as said below
- grad_out: bfloat16 [4, 2048, 2560], P('dp', 'seq'), may hold values from -12 to 12
- decay_log: float32 [40], replicated, may hold values from -16 to 1
- skip_gain: float32 [40], replicated, may hold values from 0.5 to 1.5
- codec_bias: float32 [40, 1024], replicated, may hold values from -1.75 to 1.75
- fret_bias: float32 [40, 25], replicated, may hold values from -1.75 to 1.75
- finger_damp: float32 [40, 5], replicated, may hold values from -1.4 to -0.4
Outputs:
- grad_mixer_in: bfloat16 [4, 2048, 2560], P('dp', 'seq')
- grad_step_raw: float32 [4, 40, 2048], P('dp', None, 'seq')
- grad_key_proj: bfloat16 [4, 2048, 128], P('dp', 'seq')
- grad_query_proj: bfloat16 [4, 2048, 128], P('dp', 'seq')
- grad_decay_log: float32 [40], replicated
- grad_skip_gain: float32 [40], replicated
- grad_codec_bias: float32 [40, 1024], replicated
- grad_fret_bias: float32 [40, 25], replicated
- grad_finger_damp: float32 [40, 5], replicated
The draws below stay inside these ranges and needn't reach their ends.
Inputs may be any that keep to these rules, and one draw needn't show every extreme that they name: `finger_ids`: each sequence's finger and fret ids are constant over 4 runs of positions that follow one another; the 3 positions where a run begins are drawn afresh for every sequence, one of them at a multiple of 256 where the finger changes; other neighbouring runs may share ids. `fret_ids`: constant over the same runs as finger_ids.
All inputs are finite; a program needn't handle non-finite values.
Results may differ from the reference program's by a relative error of at most 0.0057.
Values sent between devices are 32-bit elements; how exact they have to be, the bound alone decides.
A program may use at most 192 MiB of HBM per device.

```python
import math
import jax
import jax.numpy as jnp
import numpy as np
from jax import lax

H = 40
P_SIZE = 64
N = 128
V = 1024
FRETS = 25
FINGERS = 5
STRETCH = 256
NOTES = 4
TOK_DEV = 256
LENGTH = 2048
BATCH = 4


def draw_decay_log(key, part):
    pick_key, slow_key, fast_key = jax.random.split(key, 3)
    fast_share = 50
    ticket = jax.random.randint(pick_key, (H,), 0, 100)
    slow_rate = jnp.exp(jax.random.uniform(slow_key, (H,), jnp.float32, jnp.log(0.15), jnp.log(0.6))) / LENGTH
    fast_rate = jnp.exp(jax.random.uniform(fast_key, (H,), jnp.float32, jnp.log(0.5), jnp.log(2.0))) / STRETCH
    return jnp.log(jnp.where(ticket < fast_share, fast_rate, slow_rate)).astype(jnp.float32)


def draw_step_raw(key, part):
    block_key, rough_key = jax.random.split(key)
    blocks_count = LENGTH // TOK_DEV
    offsets = jax.random.uniform(block_key, (BATCH, H, blocks_count), jnp.float32, -0.5, 0.8)
    offsets = jnp.repeat(offsets, TOK_DEV, axis=2)
    rough_part = 0.6 * jax.random.normal(rough_key, (BATCH, H, LENGTH), jnp.float32)
    return jnp.clip(offsets + rough_part, -3.0, 3.0)


def draw_grad_out(key, part):
    main_key = jax.random.fold_in(key, 0)
    along_seq = 1.0 + 2.0 * jnp.arange(LENGTH, dtype=jnp.float32) / (LENGTH - 1)
    across_seq = 1.0 + 2.0 * jnp.arange(BATCH, dtype=jnp.float32) / max(BATCH - 1, 1)
    spread = across_seq[:, None, None] * along_seq[None, :, None] / 3.0
    noise_part = jnp.clip(jax.random.normal(main_key, (BATCH, LENGTH, H * P_SIZE), jnp.float32), -4.0, 4.0)
    return (noise_part * spread).astype(jnp.bfloat16)


def note_tracks(key):
    folded = jax.random.fold_in(key, 7)
    place_key, edge_key, finger_key, change_key, forced_key, fret_key = jax.random.split(folded, 6)
    sections = LENGTH // TOK_DEV
    edge_starts = TOK_DEV * jax.random.randint(edge_key, (BATCH,), 1, sections)

    def one_row(row_key, edge_at):
        others = jax.random.permutation(row_key, LENGTH - 2)[:NOTES - 2].astype(jnp.int32) + 1
        others = others + (others >= edge_at).astype(jnp.int32)
        change_flags = jnp.zeros((LENGTH,), jnp.int32).at[others].set(1).at[edge_at].set(1)
        edge_note = 1 + jnp.sum((others < edge_at).astype(jnp.int32))
        return (jnp.cumsum(change_flags).astype(jnp.int32), edge_note.astype(jnp.int32))
    note_index, edge_note = jax.vmap(one_row)(jax.random.split(place_key, BATCH), edge_starts)
    first_finger = jax.random.randint(finger_key, (BATCH, 1), 0, FINGERS)
    free_steps = jax.random.randint(change_key, (BATCH, NOTES - 1), 0, FINGERS)
    forced_steps = jax.random.randint(forced_key, (BATCH, NOTES - 1), 1, FINGERS)
    note_number = jnp.arange(1, NOTES, dtype=jnp.int32)
    steps_taken = jnp.where(note_number[None, :] == edge_note[:, None], forced_steps, free_steps)
    offsets = jnp.concatenate([jnp.zeros((BATCH, 1), jnp.int32), jnp.cumsum(steps_taken, axis=1).astype(jnp.int32)], axis=1)
    finger_of = (first_finger + offsets) % FINGERS
    fret_of = jax.random.randint(fret_key, (BATCH, NOTES), 0, FRETS)
    fingers = jnp.take_along_axis(finger_of, note_index, axis=1).astype(jnp.int32)
    frets = jnp.take_along_axis(fret_of, note_index, axis=1).astype(jnp.int32)
    return (fingers, frets)


def draw_finger_ids(key, part):
    return note_tracks(key)[0]


def draw_fret_ids(key, part):
    return note_tracks(key)[1]


def plant(entries, key, least, top_value):
    shape = entries.shape
    place = [jax.random.randint(jax.random.fold_in(key, axis), (), 0, shape[axis]) for axis in range(len(shape))]
    entries = entries.at[tuple(place)].set(least)
    longest = shape.index(max(shape))
    place[longest] = (place[longest] + 1) % shape[longest]
    return entries.at[tuple(place)].set(top_value)


def steps_of(own_key, dims, shards, smallest, top_value):
    gain, own = 1.0, jax.random.fold_in(own_key, 6)
    for axis_at, blocks in shards:
        heights = jnp.exp(jax.random.uniform(jax.random.fold_in(own, axis_at), (blocks,), jnp.float32, smallest / len(shards), top_value / len(shards)))
        gain = gain * jnp.repeat(heights, dims[axis_at] // blocks).reshape([-1 if axis == axis_at else 1 for axis in range(len(dims))])
    return gain


def cumulative_ranks(amount, skew):
    loads = [(1 << 20) // math.isqrt(standing ** skew) + 1 for standing in range(1, amount + 1)]
    width = 1 + sum(loads) // (1 << 30)
    return np.cumsum(np.array([max(1, weight // width) for weight in loads]))


def ranked_ids(key, shape, count, slope):
    grid = cumulative_ranks(count, slope)
    lot = jax.random.randint(jax.random.fold_in(key, 1), shape, 0, int(grid[count - 1]))
    grade = jnp.searchsorted(jnp.asarray(grid, jnp.int32), lot, side="right")
    return jax.random.permutation(jax.random.fold_in(key, 2), count)[grade].astype(jnp.int32)


def gaussian(stream_key, extent, width, bound, pieces=(), held_as=jnp.bfloat16):
    gain = steps_of(stream_key, extent, pieces, -0.22, 0.18) if pieces else 1.0
    result = jax.random.normal(stream_key, extent, jnp.float32) * width * gain
    return jnp.minimum(jnp.maximum(result, -bound), bound).astype(held_as)


def setup_inputs(seed: int = 0) -> dict:
    splits = jax.random.split(jax.random.key(seed), 14)
    return {
        "mixer_in": gaussian(splits[0], (BATCH, LENGTH, H * P_SIZE), 1.0, 6.0, ((0, 4), (1, 8))),
        "step_raw": draw_step_raw(jax.random.fold_in(splits[13], 71), 0),
        "key_proj": gaussian(splits[2], (BATCH, LENGTH, N), ((N ** 0.5 * (STRETCH * LENGTH) ** 0.25) ** -0.5), 0.3125, ((0, 4), (1, 8))),
        "query_proj": gaussian(splits[3], (BATCH, LENGTH, N), ((N ** 0.5 * (STRETCH * LENGTH) ** 0.25) ** -0.5), 0.3125, ((0, 4), (1, 8))),
        "codec_ids": plant(ranked_ids(splits[4], (BATCH, LENGTH), V, 2), jax.random.fold_in(splits[4], 3), 0, V - 1).astype(jnp.int32),
        "finger_ids": draw_finger_ids(jax.random.fold_in(splits[13], 71), 0),
        "fret_ids": draw_fret_ids(jax.random.fold_in(splits[13], 71), 0),
        "grad_out": draw_grad_out(jax.random.fold_in(splits[13], 71), 0),
        "decay_log": draw_decay_log(jax.random.fold_in(splits[13], 71), 0),
        "skip_gain": jnp.clip(jax.random.uniform(splits[9], (H,), jnp.float32, 0.5, 1.5), 0.5, 1.5),
        "codec_bias": gaussian(splits[10], (H, V), 0.3, 1.75, (), jnp.float32),
        "fret_bias": gaussian(splits[11], (H, FRETS), 0.3, 1.75, (), jnp.float32),
        "finger_damp": jnp.clip(jax.random.uniform(splits[12], (H, FINGERS), jnp.float32, -1.4, -0.4), -1.4, -0.4),
    }


block_heads = 8


def product(form, left, right):
    return jnp.einsum(form, left.astype(jnp.float32), right.astype(jnp.float32), precision=lax.Precision.HIGHEST)


def combine(earlier, later):
    return (earlier[0] + later[0], jnp.exp(later[0])[:, None, None] * earlier[1] + later[1])


def advance(carry, parts):
    return jnp.exp(parts[0])[:, None, None] * carry + parts[1], carry


def stretch_state(mixer_stretch, key_stretch, step_stretch, cum_stretch):
    length = mixer_stretch.shape[0]
    head_count = step_stretch.shape[0]
    tail_weight = jnp.exp(cum_stretch[:, -1:] - cum_stretch) * step_stretch
    weighted = (mixer_stretch.reshape(length, head_count, -1) * tail_weight.T[:, :, None]).astype(jnp.bfloat16)
    return product('lhp,ln->hpn', weighted, key_stretch)


def stretch_pull(grad_stretch, query_stretch, cum_stretch):
    length = grad_stretch.shape[0]
    head_count = cum_stretch.shape[0]
    weighted = (grad_stretch.reshape(length, head_count, -1) * jnp.exp(cum_stretch).T[:, :, None]).astype(jnp.bfloat16)
    return product('lhp,ln->hpn', weighted, query_stretch)


def stretch_grads(mixer_stretch, key_stretch, query_stretch, grad_stretch, step_stretch, cum_stretch, state_in, state_grad, skip_gain):
    length, feature_width = mixer_stretch.shape
    head_count = step_stretch.shape[0]
    groups = head_count // block_heads
    head_dim = feature_width // head_count
    state_dim = key_stretch.shape[1]
    row_index = jnp.arange(length)
    causal = row_index[:, None] >= row_index[None, :]
    gram_block = jnp.dot(query_stretch, key_stretch.T, preferred_element_type=jnp.float32)
    query_wide = query_stretch.astype(jnp.float32)

    def one_group(carry, parts):
        gram_grad, query_extra, key_extra = carry
        mixer_group, grad_group, step_group, cum_group, state_group, pull_group, skip_group = parts
        gap_log = cum_group[:, :, None] - cum_group[:, None, :]
        decay_part = jnp.exp(jnp.where(causal[None], gap_log, -jnp.inf))
        step_cols = step_group[:, None, :]
        weights = (gram_block[None] * decay_part * step_cols).astype(jnp.bfloat16)
        diag_grad = product('hij,ihp->jhp', weights, grad_group)
        grad_weights = product('ihp,jhp->hij', grad_group, mixer_group)
        masked = grad_weights * decay_part
        gram_grad = gram_grad + jnp.sum(masked * step_cols, axis=0)
        grad_step = jnp.sum(masked * gram_block[None], axis=1)
        row_cross = jnp.sum(masked * gram_block[None] * step_cols, axis=2)
        grad_cum = row_cross - step_group * grad_step
        state_low = state_group.astype(jnp.bfloat16)
        state_read = product('ihp,hpn->hin', grad_group, state_low)
        rise_factor = jnp.exp(cum_group)
        query_extra = query_extra + jnp.sum(rise_factor[:, :, None] * state_read, axis=0)
        grad_cum = grad_cum + rise_factor * jnp.sum(state_read * query_wide[None], axis=2)
        block_total = cum_group[:, -1]
        tail_decay = jnp.exp(block_total[:, None] - cum_group)
        tail_weight = tail_decay * step_group
        grad_low = pull_group.astype(jnp.bfloat16)
        pulled_rows = product('ln,hpn->lhp', key_stretch, grad_low)
        grad_tail = jnp.sum(mixer_group.astype(jnp.float32) * pulled_rows, axis=2).T
        mixed_state = product('lhp,hpn->hln', mixer_group, grad_low)
        key_extra = key_extra + jnp.sum(tail_weight[:, :, None] * mixed_state, axis=0)
        tail_grad = grad_tail * tail_weight
        total_grad = jnp.sum(tail_grad, axis=1) + jnp.exp(block_total) * jnp.sum(pull_group * state_group, axis=(1, 2))
        grad_cum = grad_cum - tail_grad
        grad_cum = grad_cum.at[:, -1].add(total_grad)
        grad_step = grad_step + grad_tail * tail_decay
        grad_mixer = diag_grad + tail_weight.T[:, :, None] * pulled_rows + skip_group[None, :, None] * grad_group.astype(jnp.float32)
        return (gram_grad, query_extra, key_extra), (grad_mixer, grad_step, grad_cum)

    parts = (
        mixer_stretch.reshape(length, groups, block_heads, head_dim).transpose(1, 0, 2, 3),
        grad_stretch.reshape(length, groups, block_heads, head_dim).transpose(1, 0, 2, 3),
        step_stretch.reshape(groups, block_heads, length),
        cum_stretch.reshape(groups, block_heads, length),
        state_in.reshape(groups, block_heads, head_dim, state_dim),
        state_grad.reshape(groups, block_heads, head_dim, state_dim),
        skip_gain.reshape(groups, block_heads),
    )
    start = (jnp.zeros((length, length), jnp.float32), jnp.zeros((length, state_dim), jnp.float32), jnp.zeros((length, state_dim), jnp.float32))
    (gram_grad, query_extra, key_extra), (mixer_grads, step_grads, cum_grads) = lax.scan(one_group, start, parts)
    gram_low = gram_grad.astype(jnp.bfloat16)
    grad_query = jnp.dot(gram_low, key_stretch, preferred_element_type=jnp.float32) + query_extra
    grad_key = jnp.dot(gram_low.T, query_stretch, preferred_element_type=jnp.float32) + key_extra
    grad_mixer = mixer_grads.transpose(1, 0, 2, 3).reshape(length, feature_width)
    return grad_mixer, grad_key, grad_query, step_grads.reshape(head_count, length), cum_grads.reshape(head_count, length)


def reference(mixer_in, step_raw, key_proj, query_proj, codec_ids, finger_ids, fret_ids, grad_out, decay_log, skip_gain, codec_bias, fret_bias, finger_damp):
    stretches = LENGTH // STRETCH
    feature_width = H * P_SIZE
    decay_rate = jnp.exp(decay_log)
    empty_state = jnp.zeros((H, P_SIZE, N), jnp.float32)

    def one_sequence(parts):
        mixer_row, step_row, key_row, query_row, codec_row, finger_row, fret_row, grad_row = parts
        prior_finger = jnp.concatenate([finger_row[:1], finger_row[:-1]])
        prior_fret = jnp.concatenate([fret_row[:1], fret_row[:-1]])
        onset_mask = ((finger_row != prior_finger) | (fret_row != prior_fret)).astype(jnp.float32)
        pre_step = step_row + codec_bias[:, codec_row] + fret_bias[:, fret_row]
        step_size = jax.nn.softplus(pre_step)
        damping = jax.nn.softplus(finger_damp)[:, finger_row]
        log_decay = -decay_rate[:, None] * step_size - onset_mask[None, :] * damping
        step_blocks = step_size.reshape(H, stretches, STRETCH).transpose(1, 0, 2)
        cum_blocks = jnp.cumsum(log_decay.reshape(H, stretches, STRETCH).transpose(1, 0, 2), axis=2)
        mixer_blocks = mixer_row.reshape(stretches, STRETCH, feature_width)
        grad_blocks = grad_row.reshape(stretches, STRETCH, feature_width)
        key_blocks = key_row.reshape(stretches, STRETCH, N)
        query_blocks = query_row.reshape(stretches, STRETCH, N)
        totals = cum_blocks[:, :, -1]
        states = lax.map(lambda items: stretch_state(*items), (mixer_blocks, key_blocks, step_blocks, cum_blocks))
        block_pulls = lax.map(lambda items: stretch_pull(*items), (grad_blocks, query_blocks, cum_blocks))
        state_ins = lax.scan(advance, empty_state, (totals, states))[1]
        state_grads = lax.scan(advance, empty_state, (totals, block_pulls), reverse=True)[1]
        outcome = lax.map(lambda items: stretch_grads(*items, skip_gain), (mixer_blocks, key_blocks, query_blocks, grad_blocks, step_blocks, cum_blocks, state_ins, state_grads))
        grad_mixer, grad_key, grad_query, grad_step, grad_cum = outcome
        grad_log = jnp.flip(jnp.cumsum(jnp.flip(grad_cum, 2), 2), 2)
        grad_log = grad_log.transpose(1, 0, 2).reshape(H, LENGTH)
        grad_step = grad_step.transpose(1, 0, 2).reshape(H, LENGTH)
        grad_pre = (grad_step - decay_rate[:, None] * grad_log) * jax.nn.sigmoid(pre_step)
        grad_decay = -decay_rate * jnp.sum(step_size * grad_log, axis=1)
        onset_term = jax.ops.segment_sum((-(onset_mask[None, :] * grad_log)).T, finger_row, num_segments=FINGERS).T
        grad_damp = onset_term * jax.nn.sigmoid(finger_damp)
        grad_codec = jax.ops.segment_sum(grad_pre.T, codec_row, num_segments=V).T
        grad_fret = jax.ops.segment_sum(grad_pre.T, fret_row, num_segments=FRETS).T
        grad_skip = product('lhp,lhp->h', mixer_row.reshape(LENGTH, H, P_SIZE), grad_row.reshape(LENGTH, H, P_SIZE))
        return (grad_mixer.reshape(LENGTH, feature_width).astype(jnp.bfloat16), grad_pre,
                grad_key.reshape(LENGTH, N).astype(jnp.bfloat16), grad_query.reshape(LENGTH, N).astype(jnp.bfloat16),
                grad_decay, grad_skip, grad_codec, grad_fret, grad_damp)

    results = lax.map(one_sequence, (mixer_in, step_raw, key_proj, query_proj, codec_ids, finger_ids, fret_ids, grad_out))
    grad_scale = (BATCH * LENGTH) ** -0.5
    grad_decay = jnp.sum(results[4], axis=0) * grad_scale
    grad_skip = jnp.sum(results[5], axis=0) * grad_scale
    grad_codec = jnp.sum(results[6], axis=0) * grad_scale
    grad_fret = jnp.sum(results[7], axis=0) * grad_scale
    grad_damp = jnp.sum(results[8], axis=0) * grad_scale
    return (results[0], results[1], results[2], results[3], grad_decay, grad_skip, grad_codec, grad_fret, grad_damp)
```

```python
import functools

import jax
import jax.numpy as jnp
from jax import lax
from jax.experimental import pallas as pl
from jax.experimental.pallas import tpu as pltpu
from jax.sharding import PartitionSpec as P

STRETCH = 256
LAG = 2
MESH = pl.DeviceIdType.MESH


def shifted(value, axis, by):
    count = lax.axis_size(axis)
    pairs = [(i, i + by) for i in range(count) if 0 <= i + by < count]
    return lax.ppermute(value, axis, pairs)


def dot_nn(left, right):
    return jnp.dot(left, right, preferred_element_type=jnp.float32)


def dot_nt(left, right):
    return lax.dot_general(
        left, right, (((1,), (1,)), ((), ())), preferred_element_type=jnp.float32
    )


def dot_tn(left, right):
    return lax.dot_general(
        left, right, (((0,), (0,)), ((), ())), preferred_element_type=jnp.float32
    )


def mixer_kernel(
    count,
    pairs,
    head_dim,
    x_ref,
    g_ref,
    key_ref,
    query_ref,
    key_t_ref,
    query_t_ref,
    cum_row_ref,
    cols_ref,
    total_ref,
    skip_ref,
    mix_ref,
    gkey_ref,
    gquery_ref,
    row_cross_ref,
    step_col_ref,
    cum_col_ref,
    tail_col_ref,
    meet_ref,
    skip_sum_ref,
    gram_ref,
    ggram_ref,
    qextra_ref,
    kextra_ref,
    diag_ref,
    s_ref,
    p_ref,
    e_ref,
    b_ref,
    fo_ref,
    bo_ref,
    fsend,
    frecv,
    bsend,
    brecv,
):
    me = lax.axis_index("seq")
    last = count - 1
    wide = 2 * head_dim
    length = key_ref.shape[0]
    barrier = pltpu.get_barrier_semaphore()

    @pl.when(me > 0)
    def _():
        pl.semaphore_signal(barrier, inc=1, device_id={"seq": me - 1}, device_id_type=MESH)

    @pl.when(me < last)
    def _():
        pl.semaphore_signal(barrier, inc=1, device_id={"seq": me + 1}, device_id_type=MESH)

    @pl.when(jnp.logical_and(me > 0, me < last))
    def _():
        pl.semaphore_wait(barrier, 2)

    @pl.when(jnp.logical_or(me == 0, me == last))
    def _():
        pl.semaphore_wait(barrier, 1)

    def fcopy(c):
        return pltpu.make_async_remote_copy(
            src_ref=fo_ref.at[c],
            dst_ref=e_ref.at[c],
            send_sem=fsend.at[c],
            recv_sem=frecv.at[c],
            device_id={"seq": me + 1},
            device_id_type=MESH,
        )

    def bcopy(c):
        return pltpu.make_async_remote_copy(
            src_ref=bo_ref.at[c],
            dst_ref=b_ref.at[c],
            send_sem=bsend.at[c],
            recv_sem=brecv.at[c],
            device_id={"seq": me - 1},
            device_id_type=MESH,
        )

    gram_ref[...] = dot_nt(key_ref[...], query_ref[...])
    ggram_ref[...] = jnp.zeros_like(ggram_ref)
    qextra_ref[...] = jnp.zeros_like(qextra_ref)
    kextra_ref[...] = jnp.zeros_like(kextra_ref)
    step_col_ref[...] = jnp.zeros_like(step_col_ref)
    cum_col_ref[...] = jnp.zeros_like(cum_col_ref)
    tail_col_ref[...] = jnp.zeros_like(tail_col_ref)

    def lanes(c):
        return pl.ds(pl.multiple_of(c * wide, wide), wide)

    def halves(cols, at):
        side = lax.broadcasted_iota(jnp.int32, (length, wide), 1)
        return jnp.where(side < head_dim, cols[:, at : at + 1], cols[:, at + 1 : at + 2])

    def put(ref, head, col):
        side = lax.broadcasted_iota(jnp.int32, ref.shape, 1)
        ref[...] = jnp.where(side == head, col, ref[...])

    def own(c):
        cols = cols_ref[c]
        x = x_ref[:, lanes(c)].astype(jnp.float32)
        g = g_ref[:, lanes(c)].astype(jnp.float32)
        s_ref[c] = dot_nn(key_t_ref[...], (x * halves(cols, 4)).astype(jnp.bfloat16))
        p_ref[c] = dot_nn(query_t_ref[...], (g * halves(cols, 2)).astype(jnp.bfloat16))
        skip_sum_ref[c] = jnp.sum(x * g, axis=0, keepdims=True)

    def inside(c):
        cols = cols_ref[c]
        x = x_ref[:, lanes(c)]
        g = g_ref[:, lanes(c)]
        lower = lax.broadcasted_iota(jnp.int32, (length, length), 0) <= lax.broadcasted_iota(
            jnp.int32, (length, length), 1
        )
        gram = gram_ref[...]
        added = None
        parts = []
        for k in range(2):
            span = slice(k * head_dim, (k + 1) * head_dim)
            xh, gh = x[:, span], g[:, span]
            gap = cum_row_ref[c, k : k + 1, :] - cols[:, k : k + 1]
            decay = jnp.exp(jnp.where(lower, gap, -1e30))
            step = cols[:, 6 + k : 7 + k]
            weights = ((gram * decay) * step).astype(jnp.bfloat16)
            parts.append(dot_nn(weights, gh))
            masked = dot_nt(xh, gh) * decay
            cross = masked * gram
            put(step_col_ref, 2 * c + k, jnp.sum(cross, axis=1, keepdims=True))
            row_cross_ref[c, k : k + 1, :] = jnp.sum(cross * step, axis=0, keepdims=True)
            masked = masked * step
            added = masked if added is None else added + masked
        ggram_ref[...] += added
        diag_ref[:, lanes(c)] = jnp.concatenate(parts, axis=1) + skip_ref[c] * g.astype(jnp.float32)

    def forward(c):
        @pl.when(me > 0)
        def _():
            fcopy(c).wait_recv()

        @pl.when(me == 0)
        def _():
            e_ref[c] = jnp.zeros(e_ref.shape[1:], jnp.float32)

        @pl.when(me < last)
        def _():
            fo_ref[c] = total_ref[c] * e_ref[c] + s_ref[c]
            fcopy(c).start()

    def backward(c):
        @pl.when(me < last)
        def _():
            bcopy(c).wait_recv()

        @pl.when(me == last)
        def _():
            b_ref[c] = jnp.zeros(b_ref.shape[1:], jnp.float32)

        @pl.when(me > 0)
        def _():
            bo_ref[c] = total_ref[c] * b_ref[c] + p_ref[c]
            bcopy(c).start()

    def outside(c):
        cols = cols_ref[c]
        x = x_ref[:, lanes(c)]
        g = g_ref[:, lanes(c)]
        entering = e_ref[c]
        leaving = b_ref[c]
        state_low = entering.astype(jnp.bfloat16)
        grad_low = leaving.astype(jnp.bfloat16)
        meet_ref[c] = jnp.sum(entering * leaving, axis=0, keepdims=True)
        pulled = dot_nn(key_ref[...], grad_low)
        mix_ref[:, lanes(c)] = (diag_ref[:, lanes(c)] + halves(cols, 4) * pulled).astype(jnp.bfloat16)
        key_wide = key_ref[...].astype(jnp.float32)
        query_wide = query_ref[...].astype(jnp.float32)
        qadd, kadd = None, None
        for k in range(2):
            span = slice(k * head_dim, (k + 1) * head_dim)
            read = dot_nt(g[:, span], state_low[:, span]) * cols[:, 2 + k : 3 + k]
            mixed = dot_nt(x[:, span], grad_low[:, span])
            tail = jnp.sum(mixed * key_wide, axis=1, keepdims=True)
            put(tail_col_ref, 2 * c + k, tail)
            put(cum_col_ref, 2 * c + k, jnp.sum(read * query_wide, axis=1, keepdims=True))
            mixed = mixed * cols[:, 4 + k : 5 + k]
            qadd = read if qadd is None else qadd + read
            kadd = mixed if kadd is None else kadd + mixed
        qextra_ref[...] += qadd
        kextra_ref[...] += kadd

    def within(c, work):
        @pl.when(jnp.logical_and(c >= 0, c < pairs))
        def _():
            work(c)

    def tick(t, carry):
        within(t, own)
        within(t - LAG * me, forward)
        within(t - LAG * (last - me), backward)
        within(t, inside)
        within(t - LAG * jnp.maximum(me, last - me), outside)
        return carry

    lax.fori_loop(0, pairs + LAG * last, tick, 0)
    low = ggram_ref[...].astype(jnp.bfloat16)
    gquery_ref[...] = (dot_tn(low, key_ref[...]) + qextra_ref[...]).astype(jnp.bfloat16)
    gkey_ref[...] = (dot_nn(low, query_ref[...]) + kextra_ref[...]).astype(jnp.bfloat16)

    def drain(c, carry):
        @pl.when(me < last)
        def _():
            fcopy(c).wait_send()

        @pl.when(me > 0)
        def _():
            bcopy(c).wait_send()

        return carry

    lax.fori_loop(0, pairs, drain, 0)


def mixer_call(x, g, key, query, cum, step, skip_gain):
    length, width = x.shape
    heads = cum.shape[0]
    head_dim = width // heads
    state = key.shape[1]
    pairs = heads // 2
    wide = 2 * head_dim
    count = lax.axis_size("seq")
    total = cum[:, -1:]
    rise = jnp.exp(cum)
    tail_weight = jnp.exp(total - cum) * step
    cols = jnp.stack([cum, rise, tail_weight, step])
    cols = cols.reshape(4, pairs, 2, length).transpose(1, 3, 0, 2).reshape(pairs, length, 8)
    total_wide = jnp.broadcast_to(jnp.exp(total), (heads, head_dim)).reshape(pairs, 1, wide)
    skip_wide = jnp.broadcast_to(skip_gain[:, None], (heads, head_dim)).reshape(pairs, 1, wide)
    f32 = jnp.float32
    column = jax.ShapeDtypeStruct((length, 128), f32)
    line = jax.ShapeDtypeStruct((pairs, 1, wide), f32)
    small = jax.ShapeDtypeStruct((length, state), jnp.bfloat16)
    vmem = pl.BlockSpec(memory_space=pltpu.VMEM)
    states = pltpu.VMEM((pairs, state, wide), f32)
    sems = pltpu.SemaphoreType.DMA((pairs,))
    return pl.pallas_call(
        functools.partial(mixer_kernel, count, pairs, head_dim),
        out_shape=[
            jax.ShapeDtypeStruct((length, width), jnp.bfloat16),
            small,
            small,
            jax.ShapeDtypeStruct((pairs, 2, length), f32),
            column,
            column,
            column,
            line,
            line,
        ],
        in_specs=[vmem] * 10,
        out_specs=[vmem] * 9,
        scratch_shapes=[
            pltpu.VMEM((length, length), f32),
            pltpu.VMEM((length, length), f32),
            pltpu.VMEM((length, state), f32),
            pltpu.VMEM((length, state), f32),
            pltpu.VMEM((length, width), f32),
        ]
        + [states] * 6
        + [sems] * 4,
        compiler_params=pltpu.CompilerParams(
            collective_id=0, has_side_effects=True, vmem_limit_bytes=56 * 1024 * 1024
        ),
    )(
        x,
        g,
        key,
        query,
        key.T,
        query.T,
        cum.reshape(pairs, 2, length),
        cols,
        total_wide,
        skip_wide,
    )


def sum_kernel(stages, in_ref, out_ref, got_ref, send, recv):
    barrier = pltpu.get_barrier_semaphore()

    def partner(axis, bit):
        me = lax.axis_index(axis)
        return {axis: me + bit - 2 * bit * (lax.div(me, bit) % 2)}

    for axis, bit in stages:
        pl.semaphore_signal(barrier, inc=1, device_id=partner(axis, bit), device_id_type=MESH)
    pl.semaphore_wait(barrier, len(stages))
    out_ref[0] = in_ref[...]
    for at, (axis, bit) in enumerate(stages):
        copy = pltpu.make_async_remote_copy(
            src_ref=out_ref.at[at],
            dst_ref=got_ref.at[at],
            send_sem=send.at[at],
            recv_sem=recv.at[at],
            device_id=partner(axis, bit),
            device_id_type=MESH,
        )
        copy.start()
        copy.wait()
        out_ref[at + 1] = out_ref[at] + got_ref[at]


def summed(value):
    stages = []
    for axis in ("dp", "seq"):
        size, bit = lax.axis_size(axis), 1
        while bit < size:
            stages.append((axis, bit))
            bit *= 2
    n = len(stages)
    vmem = pl.BlockSpec(memory_space=pltpu.VMEM)

    def body(in_ref, final_ref, out_ref, got_ref, send, recv):
        sum_kernel(stages, in_ref, out_ref, got_ref, send, recv)
        final_ref[...] = out_ref[n]

    return pl.pallas_call(
        body,
        out_shape=jax.ShapeDtypeStruct(value.shape, value.dtype),
        in_specs=[vmem],
        out_specs=vmem,
        scratch_shapes=[
            pltpu.VMEM((n + 1, *value.shape), value.dtype),
            pltpu.VMEM((n, *value.shape), value.dtype),
            pltpu.SemaphoreType.DMA((n,)),
            pltpu.SemaphoreType.DMA((n,)),
        ],
        compiler_params=pltpu.CompilerParams(collective_id=1, has_side_effects=True),
    )(value)


def shards(
    mixer_in,
    step_raw,
    key_proj,
    query_proj,
    codec_ids,
    finger_ids,
    fret_ids,
    grad_out,
    decay_log,
    skip_gain,
    codec_bias,
    fret_bias,
    finger_damp,
):
    tokens = mixer_in.shape[1]
    head_count = decay_log.shape[0]
    highest = lax.Precision.HIGHEST
    fingers = finger_ids[0]
    frets = fret_ids[0]
    codec_row = codec_ids[0]
    latest = jnp.stack([fingers[-1], frets[-1]])
    before = shifted(latest, "seq", 1)
    prior_finger = jnp.concatenate([before[0:1], fingers[:-1]])
    prior_fret = jnp.concatenate([before[1:2], frets[:-1]])
    position = lax.axis_index("seq") * tokens + jnp.arange(tokens, dtype=jnp.int32)
    changed = ((fingers != prior_finger) | (frets != prior_fret)).astype(jnp.float32)
    onset_mask = jnp.where(position == 0, 0.0, changed)
    codec_hot = (
        jnp.arange(codec_bias.shape[1], dtype=jnp.int32)[:, None] == codec_row[None, :]
    ).astype(jnp.float32)
    fret_hot = (jnp.arange(fret_bias.shape[1], dtype=jnp.int32)[:, None] == frets[None, :]).astype(
        jnp.float32
    )
    finger_hot = (
        jnp.arange(finger_damp.shape[1], dtype=jnp.int32)[:, None] == fingers[None, :]
    ).astype(jnp.float32)
    pre_step = (
        step_raw[0]
        + jnp.dot(codec_bias, codec_hot, precision=highest)
        + jnp.dot(fret_bias, fret_hot, precision=highest)
    )
    step_size = jax.nn.softplus(pre_step)
    damping = jnp.dot(jax.nn.softplus(finger_damp), finger_hot, precision=highest)
    decay_rate = jnp.exp(decay_log)
    log_decay = -decay_rate[:, None] * step_size - onset_mask[None, :] * damping
    cum = jnp.cumsum(log_decay, axis=1)
    (
        grad_mixer,
        grad_key,
        grad_query,
        row_cross,
        step_col,
        read_col,
        tail_col,
        meet,
        skip_sum,
    ) = mixer_call(mixer_in[0], grad_out[0], key_proj[0], query_proj[0], cum, step_size, skip_gain)
    own_step = step_col[:, :head_count].T
    grad_tail = tail_col[:, :head_count].T
    total = cum[:, -1:]
    tail_decay = jnp.exp(total - cum)
    tail_grad = grad_tail * tail_decay * step_size
    total_grad = jnp.sum(tail_grad, axis=1) + jnp.exp(total[:, 0]) * jnp.sum(
        meet.reshape(head_count, -1), axis=1
    )
    grad_cum = (
        row_cross.reshape(head_count, tokens)
        - step_size * own_step
        + read_col[:, :head_count].T
        - tail_grad
    )
    grad_cum = grad_cum.at[:, -1].add(total_grad)
    grad_step = own_step + grad_tail * tail_decay
    grad_log = jnp.flip(jnp.cumsum(jnp.flip(grad_cum, 1), 1), 1)
    grad_pre = (grad_step - decay_rate[:, None] * grad_log) * jax.nn.sigmoid(pre_step)
    grad_decay = -decay_rate * jnp.sum(step_size * grad_log, axis=1)
    grad_damp = jnp.dot(
        -(onset_mask[None, :] * grad_log), finger_hot.T, precision=highest
    ) * jax.nn.sigmoid(finger_damp)
    grad_codec = jnp.dot(grad_pre, codec_hot.T, precision=highest)
    grad_fret = jnp.dot(grad_pre, fret_hot.T, precision=highest)
    grad_skip = jnp.sum(skip_sum.reshape(head_count, -1), axis=1)
    vocab, frets_n, fingers_n = codec_bias.shape[1], fret_bias.shape[1], finger_damp.shape[1]
    packed = jnp.concatenate(
        [grad_codec, grad_fret, grad_damp, grad_skip[:, None], grad_decay[:, None]], axis=1
    )
    packed = jnp.pad(packed, ((0, 0), (0, -packed.shape[1] % 128)))
    grad_scale = (lax.axis_size("dp") * lax.axis_size("seq") * tokens) ** (-0.5)
    packed = summed(packed) * grad_scale
    a, b, c = vocab, vocab + frets_n, vocab + frets_n + fingers_n
    return (
        grad_mixer[None],
        grad_pre[None],
        grad_key[None],
        grad_query[None],
        packed[:, c + 1],
        packed[:, c],
        packed[:, :a],
        packed[:, a:b],
        packed[:, b:c],
    )


def solution(mesh):
    in_specs = (
        P("dp", "seq", None),
        P("dp", None, "seq"),
        P("dp", "seq", None),
        P("dp", "seq", None),
        P("dp", "seq"),
        P("dp", "seq"),
        P("dp", "seq"),
        P("dp", "seq", None),
        P(),
        P(),
        P(),
        P(),
        P(),
    )
    out_specs = (
        P("dp", "seq", None),
        P("dp", None, "seq"),
        P("dp", "seq", None),
        P("dp", "seq", None),
        P(),
        P(),
        P(),
        P(),
        P(),
    )
    return jax.shard_map(shards, mesh=mesh, in_specs=in_specs, out_specs=out_specs, check_vma=False)
```

```python
import functools

import jax
import jax.numpy as jnp
from jax import lax
from jax.experimental import pallas as pl
from jax.experimental.pallas import tpu as pltpu
from jax.sharding import PartitionSpec as P

LAG = 2
MESH = pl.DeviceIdType.MESH


def dot_nn(left, right):
    return jnp.dot(left, right, preferred_element_type=jnp.float32)


def dot_nt(left, right):
    return lax.dot_general(
        left, right, (((1,), (1,)), ((), ())), preferred_element_type=jnp.float32
    )


def dot_tn(left, right):
    return lax.dot_general(
        left, right, (((0,), (0,)), ((), ())), preferred_element_type=jnp.float32
    )


def pieces(value):
    high = value.astype(jnp.bfloat16)
    rest = value - high.astype(jnp.float32)
    middle = rest.astype(jnp.bfloat16)
    low = (rest - middle.astype(jnp.float32)).astype(jnp.bfloat16)
    return high, middle, low


def exact(form, value, ones):
    high, middle, low = pieces(value)
    return form(low, ones) + form(middle, ones) + form(high, ones)


def soft(value):
    return jnp.maximum(value, 0.0) + jnp.log1p(jnp.exp(-jnp.abs(value)))


def logistic(value):
    return 1.0 / (1.0 + jnp.exp(-value))


FINGER_LANE, DECAY_LANE, SKIP_LANE = 32, 64, 65


def mixer_kernel(
    count,
    pairs,
    head_dim,
    stages,
    scale,
    x_ref,
    g_ref,
    key_ref,
    query_ref,
    raw_ref,
    codec_ref,
    finger_ref,
    fret_ref,
    table_ref,
    small_ref,
    decay_ref,
    skip_ref,
    mix_ref,
    gstep_ref,
    gkey_ref,
    gquery_ref,
    gcodec_ref,
    gsmall_ref,
    gram_ref,
    ggram_ref,
    qextra_ref,
    kextra_ref,
    diag_ref,
    s_ref,
    p_ref,
    e_ref,
    b_ref,
    fo_ref,
    bo_ref,
    rows_ref,
    cols_ref,
    pre_ref,
    row_cross_ref,
    step_col_ref,
    cum_col_ref,
    tail_col_ref,
    meet_ref,
    skip_sum_ref,
    before_ref,
    key_t_ref,
    query_t_ref,
    all_ref,
    half_ref,
    got_half_ref,
    quarter_ref,
    got_ref,
    join_half_ref,
    join_ref,
    fsend,
    frecv,
    bsend,
    brecv,
    isend,
    irecv,
    ssend,
    srecv,
):
    me = lax.axis_index("seq")
    last = count - 1
    wide = 2 * head_dim
    heads = 2 * pairs
    length = key_ref.shape[0]
    barrier = pltpu.get_barrier_semaphore()

    def bit_of(axis, bit):
        return (lax.axis_index(axis) // bit) % 2

    def partner(axis, bit):
        return {axis: lax.axis_index(axis) + bit - 2 * bit * bit_of(axis, bit)}

    others = [stage for stage in stages if stage != ("seq", 1)]

    @pl.when(me > 0)
    def _():
        pl.semaphore_signal(barrier, inc=1, device_id={"seq": me - 1}, device_id_type=MESH)

    @pl.when(me < last)
    def _():
        pl.semaphore_signal(barrier, inc=1, device_id={"seq": me + 1}, device_id_type=MESH)

    for stage in others:
        pl.semaphore_signal(barrier, inc=1, device_id=partner(*stage), device_id_type=MESH)

    @pl.when(jnp.logical_and(me > 0, me < last))
    def _():
        pl.semaphore_wait(barrier, 2 + len(others))

    @pl.when(jnp.logical_or(me == 0, me == last))
    def _():
        pl.semaphore_wait(barrier, 1 + len(others))

    def icopy(at):
        return pltpu.make_async_remote_copy(
            src_ref=(finger_ref, fret_ref)[at],
            dst_ref=before_ref.at[at],
            send_sem=isend.at[at],
            recv_sem=irecv.at[at],
            device_id={"seq": me + 1},
            device_id_type=MESH,
        )

    @pl.when(me < last)
    def _():
        icopy(0).start()
        icopy(1).start()

    codec_hot = (
        lax.broadcasted_iota(jnp.int32, (table_ref.shape[1], length), 0) == codec_ref[...]
    ).astype(jnp.float32).astype(jnp.bfloat16)
    small_row = lax.broadcasted_iota(jnp.int32, (128, length), 0)
    fret_hot = (small_row == fret_ref[...]).astype(jnp.float32).astype(jnp.bfloat16)
    finger_hot = (
        (small_row == finger_ref[...] + FINGER_LANE).astype(jnp.float32).astype(jnp.bfloat16)
    )
    pre_step = (
        raw_ref[0] + exact(dot_nn, table_ref[...], codec_hot) + exact(dot_nn, small_ref[...], fret_hot)
    )
    pre_ref[...] = pre_step
    step = soft(pre_step)
    damping = exact(dot_nn, soft(small_ref[...]), finger_hot)
    head_row = lax.broadcasted_iota(jnp.int32, (heads, 1), 0)
    rate = jnp.zeros((heads, 1), jnp.float32)
    for h in range(heads):
        rate = jnp.where(head_row == h, decay_ref[h], rate)
    rate = jnp.exp(rate)
    key_t_ref[...] = key_ref[...].astype(jnp.float32).T.astype(jnp.bfloat16)
    query_t_ref[...] = query_ref[...].astype(jnp.float32).T.astype(jnp.bfloat16)
    place = lax.broadcasted_iota(jnp.int32, (length, length), 0)
    other = lax.broadcasted_iota(jnp.int32, (length, length), 1)

    @pl.when(me > 0)
    def _():
        pltpu.make_async_remote_copy(
            src_ref=finger_ref,
            dst_ref=before_ref.at[0],
            send_sem=isend.at[0],
            recv_sem=irecv.at[0],
            device_id={"seq": me - 1},
            device_id_type=MESH,
        ).wait_recv()
        pltpu.make_async_remote_copy(
            src_ref=fret_ref,
            dst_ref=before_ref.at[1],
            send_sem=isend.at[1],
            recv_sem=irecv.at[1],
            device_id={"seq": me - 1},
            device_id_type=MESH,
        ).wait_recv()

    @pl.when(me == 0)
    def _():
        before_ref[0] = finger_ref[...]
        before_ref[1] = fret_ref[...]

    spot = lax.broadcasted_iota(jnp.int32, (1, length), 1)

    def changed(ref, at):
        prior = jnp.where(spot == 0, pltpu.roll(before_ref[at], 1, 1), pltpu.roll(ref[...], 1, 1))
        return (ref[...] != prior).astype(jnp.float32)

    onset = jnp.maximum(changed(finger_ref, 0), changed(fret_ref, 1))
    onset = jnp.where(spot + me * length == 0, 0.0, onset)
    log_decay = -rate * step - onset * damping
    until = (place <= other).astype(jnp.float32).astype(jnp.bfloat16)
    cum = exact(dot_nn, log_decay, until)
    rise = jnp.exp(cum)
    tail_decay = jnp.exp(cum[:, length - 1 :] - cum)
    tail_weight = tail_decay * step
    for c in range(pairs):
        both = slice(2 * c, 2 * c + 2)
        rows_ref[c, 0:2, :] = cum[both]
        rows_ref[c, 2:4, :] = rise[both]
        rows_ref[c, 4:6, :] = tail_weight[both]
        rows_ref[c, 6:8, :] = step[both]
    def fcopy(c):
        return pltpu.make_async_remote_copy(
            src_ref=fo_ref.at[c],
            dst_ref=e_ref.at[c],
            send_sem=fsend.at[c],
            recv_sem=frecv.at[c],
            device_id={"seq": me + 1},
            device_id_type=MESH,
        )

    def bcopy(c):
        return pltpu.make_async_remote_copy(
            src_ref=bo_ref.at[c],
            dst_ref=b_ref.at[c],
            send_sem=bsend.at[c],
            recv_sem=brecv.at[c],
            device_id={"seq": me - 1},
            device_id_type=MESH,
        )

    gram_ref[...] = dot_nt(key_ref[...], query_ref[...])
    ggram_ref[...] = jnp.zeros_like(ggram_ref)
    qextra_ref[...] = jnp.zeros_like(qextra_ref)
    kextra_ref[...] = jnp.zeros_like(kextra_ref)
    step_col_ref[...] = jnp.zeros_like(step_col_ref)
    cum_col_ref[...] = jnp.zeros_like(cum_col_ref)
    tail_col_ref[...] = jnp.zeros_like(tail_col_ref)

    def lanes(c):
        return pl.ds(pl.multiple_of(c * wide, wide), wide)

    def halves(cols, at):
        side = lax.broadcasted_iota(jnp.int32, (length, wide), 1)
        return jnp.where(side < head_dim, cols[:, at : at + 1], cols[:, at + 1 : at + 2])

    def put(ref, head, col):
        side = lax.broadcasted_iota(jnp.int32, ref.shape, 1)
        ref[...] = jnp.where(side == head, col, ref[...])

    lane_side = lax.broadcasted_iota(jnp.int32, (1, wide), 1)

    def whole_decay(c):
        end = cols_ref[c, length - 1 : length, :]
        return jnp.where(lane_side < head_dim, end[:, 2:3], end[:, 3:4])

    def split(ref, c, line):
        ref[pl.ds(2 * c, 1), :] = jnp.where(lane_side < head_dim, line, 0.0)
        ref[pl.ds(2 * c + 1, 1), :] = jnp.where(lane_side < head_dim, 0.0, line)

    def own(c):
        cols_ref[c] = rows_ref[c].T
        cols = cols_ref[c]
        x = x_ref[:, lanes(c)].astype(jnp.float32)
        g = g_ref[:, lanes(c)].astype(jnp.float32)
        s_ref[c] = dot_nn(key_t_ref[...], (x * halves(cols, 4)).astype(jnp.bfloat16))
        p_ref[c] = dot_nn(query_t_ref[...], (g * halves(cols, 2)).astype(jnp.bfloat16))
        split(skip_sum_ref, c, jnp.sum(x * g, axis=0, keepdims=True))

    def inside(c):
        cols = cols_ref[c]
        x = x_ref[:, lanes(c)]
        g = g_ref[:, lanes(c)]
        lower = lax.broadcasted_iota(jnp.int32, (length, length), 0) <= lax.broadcasted_iota(
            jnp.int32, (length, length), 1
        )
        gram = gram_ref[...]
        added = None
        parts = []
        for k in range(2):
            span = slice(k * head_dim, (k + 1) * head_dim)
            xh, gh = x[:, span], g[:, span]
            gap = rows_ref[c, k : k + 1, :] - cols[:, k : k + 1]
            decay = jnp.exp(jnp.where(lower, gap, -1e30))
            step = cols[:, 6 + k : 7 + k]
            weights = ((gram * decay) * step).astype(jnp.bfloat16)
            parts.append(dot_nn(weights, gh))
            masked = dot_nt(xh, gh) * decay
            cross = masked * gram
            put(step_col_ref, 2 * c + k, jnp.sum(cross, axis=1, keepdims=True))
            row_cross_ref[pl.ds(2 * c + k, 1), :] = jnp.sum(cross * step, axis=0, keepdims=True)
            masked = masked * step
            added = masked if added is None else added + masked
        ggram_ref[...] += added
        gain = jnp.where(lane_side < head_dim, skip_ref[2 * c], skip_ref[2 * c + 1])
        diag_ref[:, lanes(c)] = jnp.concatenate(parts, axis=1) + gain * g.astype(jnp.float32)

    def forward(c):
        @pl.when(me > 0)
        def _():
            fcopy(c).wait_recv()

        @pl.when(me == 0)
        def _():
            e_ref[c] = jnp.zeros(e_ref.shape[1:], jnp.float32)

        @pl.when(me < last)
        def _():
            fo_ref[c] = whole_decay(c) * e_ref[c] + s_ref[c]
            fcopy(c).start()

    def backward(c):
        @pl.when(me < last)
        def _():
            bcopy(c).wait_recv()

        @pl.when(me == last)
        def _():
            b_ref[c] = jnp.zeros(b_ref.shape[1:], jnp.float32)

        @pl.when(me > 0)
        def _():
            bo_ref[c] = whole_decay(c) * b_ref[c] + p_ref[c]
            bcopy(c).start()

    def outside(c):
        cols = cols_ref[c]
        x = x_ref[:, lanes(c)]
        g = g_ref[:, lanes(c)]
        entering = e_ref[c]
        leaving = b_ref[c]
        state_low = entering.astype(jnp.bfloat16)
        grad_low = leaving.astype(jnp.bfloat16)
        split(meet_ref, c, jnp.sum(entering * leaving, axis=0, keepdims=True))
        pulled = dot_nn(key_ref[...], grad_low)
        mix_ref[:, lanes(c)] = (diag_ref[:, lanes(c)] + halves(cols, 4) * pulled).astype(jnp.bfloat16)
        key_wide = key_ref[...].astype(jnp.float32)
        query_wide = query_ref[...].astype(jnp.float32)
        qadd, kadd = None, None
        for k in range(2):
            span = slice(k * head_dim, (k + 1) * head_dim)
            read = dot_nt(g[:, span], state_low[:, span]) * cols[:, 2 + k : 3 + k]
            mixed = dot_nt(x[:, span], grad_low[:, span])
            tail = jnp.sum(mixed * key_wide, axis=1, keepdims=True)
            put(tail_col_ref, 2 * c + k, tail)
            put(cum_col_ref, 2 * c + k, jnp.sum(read * query_wide, axis=1, keepdims=True))
            mixed = mixed * cols[:, 4 + k : 5 + k]
            qadd = read if qadd is None else qadd + read
            kadd = mixed if kadd is None else kadd + mixed
        qextra_ref[...] += qadd
        kextra_ref[...] += kadd

    def within(c, work):
        @pl.when(jnp.logical_and(c >= 0, c < pairs))
        def _():
            work(c)

    def tick(t, carry):
        within(t, own)
        within(t - LAG * me, forward)
        within(t - LAG * (last - me), backward)
        within(t, inside)
        within(t - LAG * jnp.maximum(me, last - me), outside)
        return carry

    lax.fori_loop(0, pairs + LAG * last, tick, 0)
    low = ggram_ref[...].astype(jnp.bfloat16)
    gquery_ref[...] = (dot_tn(low, key_ref[...]) + qextra_ref[...]).astype(jnp.bfloat16)
    gkey_ref[...] = (dot_nn(low, query_ref[...]) + kextra_ref[...]).astype(jnp.bfloat16)

    @pl.when(me < last)
    def _():
        icopy(0).wait_send()
        icopy(1).wait_send()

    def drain(c, carry):
        @pl.when(me < last)
        def _():
            fcopy(c).wait_send()

        @pl.when(me > 0)
        def _():
            bcopy(c).wait_send()

        return carry

    lax.fori_loop(0, pairs, drain, 0)

    own_step = step_col_ref[...].T[:heads]
    grad_tail = tail_col_ref[...].T[:heads]
    tail_grad = grad_tail * tail_weight
    meet = jnp.sum(meet_ref[...], axis=1, keepdims=True)
    total_grad = jnp.sum(tail_grad, axis=1, keepdims=True) + rise[:, length - 1 :] * meet
    grad_cum = row_cross_ref[...] - step * own_step + cum_col_ref[...].T[:heads] - tail_grad
    grad_cum = jnp.where(spot == length - 1, grad_cum + total_grad, grad_cum)
    after = (place >= other).astype(jnp.float32).astype(jnp.bfloat16)
    grad_log = exact(dot_nn, grad_cum, after)
    grad_pre = (own_step + grad_tail * tail_decay - rate * grad_log) * logistic(pre_ref[...])
    gstep_ref[0] = grad_pre
    grad_codec = exact(dot_nt, grad_pre, codec_hot)
    grad_small = exact(dot_nt, grad_pre, fret_hot) + exact(
        dot_nt, -(onset * grad_log), finger_hot
    ) * logistic(small_ref[...])
    lane = lax.broadcasted_iota(jnp.int32, (1, 128), 1)
    grad_decay = -rate * jnp.sum(step * grad_log, axis=1, keepdims=True)
    grad_skip = jnp.sum(skip_sum_ref[...], axis=1, keepdims=True)
    grad_small = jnp.where(lane == DECAY_LANE, grad_decay, grad_small)
    grad_small = jnp.where(lane == SKIP_LANE, grad_skip, grad_small)
    tall, broad = heads // 8, table_ref.shape[1] // 128 + 1
    for a in range(tall):
        for b in range(broad):
            source = grad_small if b == broad - 1 else grad_codec
            at = 0 if b == broad - 1 else 128 * b
            all_ref[a * broad + b] = source[8 * a : 8 * a + 8, at : at + 128]
    for at in range(tall * broad, all_ref.shape[0]):
        all_ref[at] = jnp.zeros(all_ref.shape[1:], jnp.float32)

    def exchange(at, stage, src, dst):
        copy = pltpu.make_async_remote_copy(
            src_ref=src,
            dst_ref=dst,
            send_sem=ssend.at[at],
            recv_sem=srecv.at[at],
            device_id=partner(*stage),
            device_id_type=MESH,
        )
        copy.start()
        copy.wait()

    half, quarter = half_ref.shape[0], quarter_ref.shape[1]
    first, second = bit_of(*stages[0]), bit_of(*stages[1])
    exchange(0, stages[0], all_ref.at[pl.ds((1 - first) * half, half)], got_half_ref)
    half_ref[...] = all_ref[pl.ds(first * half, half)] + got_half_ref[...]
    exchange(1, stages[1], half_ref.at[pl.ds((1 - second) * quarter, quarter)], got_ref.at[0])
    quarter_ref[0] = half_ref[pl.ds(second * quarter, quarter)] + got_ref[0]
    rest = len(stages) - 2
    for at in range(rest):
        exchange(2 + at, stages[2 + at], quarter_ref.at[at], got_ref.at[at + 1])
        quarter_ref[at + 1] = quarter_ref[at] + got_ref[at + 1]
    mine = pl.ds(second * quarter, quarter)
    join_half_ref[mine] = quarter_ref[rest]
    exchange(2 + rest, stages[1], quarter_ref.at[rest], join_half_ref.at[mine])
    mine = pl.ds(first * half, half)
    join_ref[mine] = join_half_ref[...]
    exchange(3 + rest, stages[0], join_half_ref, join_ref.at[mine])
    for a in range(tall):
        for b in range(broad):
            value = join_ref[a * broad + b] * scale
            if b == broad - 1:
                gsmall_ref[8 * a : 8 * a + 8, :] = value
            else:
                gcodec_ref[8 * a : 8 * a + 8, 128 * b : 128 * b + 128] = value


def shards(
    mixer_in,
    step_raw,
    key_proj,
    query_proj,
    codec_ids,
    finger_ids,
    fret_ids,
    grad_out,
    decay_log,
    skip_gain,
    codec_bias,
    fret_bias,
    finger_damp,
):
    length, width = mixer_in.shape[1:]
    heads = decay_log.shape[0]
    head_dim = width // heads
    state = key_proj.shape[2]
    vocab = codec_bias.shape[1]
    frets, fingers = fret_bias.shape[1], finger_damp.shape[1]
    pairs = heads // 2
    wide = 2 * head_dim
    count = lax.axis_size("seq")
    stages = []
    for axis in ("dp", "seq"):
        bit = 1
        while bit < lax.axis_size(axis):
            stages.append((axis, bit))
            bit *= 2
    scale = float((lax.axis_size("dp") * count * length) ** (-0.5))
    small = jnp.pad(fret_bias, ((0, 0), (0, 128 - frets))) + jnp.pad(
        finger_damp, ((0, 0), (FINGER_LANE, 128 - FINGER_LANE - fingers))
    )
    tiles = (heads // 8) * (vocab // 128 + 1)
    tiles += -tiles % 4
    f32, bf16 = jnp.float32, jnp.bfloat16
    vmem = pl.BlockSpec(memory_space=pltpu.VMEM)
    smem = pl.BlockSpec(memory_space=pltpu.SMEM)
    states = pltpu.VMEM((pairs, state, wide), f32)
    column = pltpu.VMEM((length, 128), f32)
    sems = pltpu.SemaphoreType.DMA((pairs,))
    rounds = len(stages)
    grad_mixer, grad_step, grad_key, grad_query, grad_codec, grad_small = pl.pallas_call(
        functools.partial(mixer_kernel, count, pairs, head_dim, stages, scale),
        out_shape=[
            jax.ShapeDtypeStruct((length, width), bf16),
            jax.ShapeDtypeStruct((1, heads, length), f32),
            jax.ShapeDtypeStruct((length, state), bf16),
            jax.ShapeDtypeStruct((length, state), bf16),
            jax.ShapeDtypeStruct((heads, vocab), f32),
            jax.ShapeDtypeStruct((heads, 128), f32),
        ],
        in_specs=[vmem] * 10 + [smem] * 2,
        out_specs=[vmem] * 6,
        scratch_shapes=[
            pltpu.VMEM((length, length), f32),
            pltpu.VMEM((length, length), f32),
            pltpu.VMEM((length, state), f32),
            pltpu.VMEM((length, state), f32),
            pltpu.VMEM((length, width), f32),
        ]
        + [states] * 6
        + [
            pltpu.VMEM((pairs, 8, length), f32),
            pltpu.VMEM((pairs, length, 8), f32),
            pltpu.VMEM((heads, length), f32),
            pltpu.VMEM((heads, length), f32),
            column,
            column,
            column,
            pltpu.VMEM((heads, wide), f32),
            pltpu.VMEM((heads, wide), f32),
            pltpu.VMEM((2, 1, length), jnp.int32),
            pltpu.VMEM((state, length), bf16),
            pltpu.VMEM((state, length), bf16),
            pltpu.VMEM((tiles, 8, 128), f32),
            pltpu.VMEM((tiles // 2, 8, 128), f32),
            pltpu.VMEM((tiles // 2, 8, 128), f32),
            pltpu.VMEM((rounds - 1, tiles // 4, 8, 128), f32),
            pltpu.VMEM((rounds - 1, tiles // 4, 8, 128), f32),
            pltpu.VMEM((tiles // 2, 8, 128), f32),
            pltpu.VMEM((tiles, 8, 128), f32),
        ]
        + [sems] * 4
        + [pltpu.SemaphoreType.DMA((2,))] * 2
        + [pltpu.SemaphoreType.DMA((rounds + 2,))] * 2,
        compiler_params=pltpu.CompilerParams(
            collective_id=0, has_side_effects=True, vmem_limit_bytes=56 * 1024 * 1024
        ),
    )(
        mixer_in[0],
        grad_out[0],
        key_proj[0],
        query_proj[0],
        step_raw,
        codec_ids,
        finger_ids,
        fret_ids,
        codec_bias,
        small,
        decay_log,
        skip_gain,
    )
    return (
        grad_mixer[None],
        grad_step,
        grad_key[None],
        grad_query[None],
        grad_small[:, DECAY_LANE],
        grad_small[:, SKIP_LANE],
        grad_codec,
        grad_small[:, :frets],
        grad_small[:, FINGER_LANE : FINGER_LANE + fingers],
    )


def solution(mesh):
    in_specs = (
        P("dp", "seq", None),
        P("dp", None, "seq"),
        P("dp", "seq", None),
        P("dp", "seq", None),
        P("dp", "seq"),
        P("dp", "seq"),
        P("dp", "seq"),
        P("dp", "seq", None),
        P(),
        P(),
        P(),
        P(),
        P(),
    )
    out_specs = (
        P("dp", "seq", None),
        P("dp", None, "seq"),
        P("dp", "seq", None),
        P("dp", "seq", None),
        P(),
        P(),
        P(),
        P(),
        P(),
    )
    return jax.shard_map(shards, mesh=mesh, in_specs=in_specs, out_specs=out_specs, check_vma=False)
```

```python
import functools

import jax
import jax.numpy as jnp
from jax import lax
from jax.experimental import pallas as pl
from jax.experimental.pallas import tpu as pltpu
from jax.sharding import PartitionSpec as P

LAG = 2
MESH = pl.DeviceIdType.MESH


def dot_nn(left, right):
    return jnp.dot(left, right, preferred_element_type=jnp.float32)


def dot_nt(left, right):
    return lax.dot_general(
        left, right, (((1,), (1,)), ((), ())), preferred_element_type=jnp.float32
    )


def dot_tn(left, right):
    return lax.dot_general(
        left, right, (((0,), (0,)), ((), ())), preferred_element_type=jnp.float32
    )


def pieces(value):
    high = value.astype(jnp.bfloat16)
    rest = value - high.astype(jnp.float32)
    middle = rest.astype(jnp.bfloat16)
    low = (rest - middle.astype(jnp.float32)).astype(jnp.bfloat16)
    return high, middle, low


def exact(form, value, ones):
    high, middle, low = pieces(value)
    return form(low, ones) + form(middle, ones) + form(high, ones)


def soft(value):
    return jnp.maximum(value, 0.0) + jnp.log1p(jnp.exp(-jnp.abs(value)))


def logistic(value):
    return 1.0 / (1.0 + jnp.exp(-value))


FINGER_LANE, DECAY_LANE, SKIP_LANE = 32, 64, 65


def mixer_kernel(
    count,
    pairs,
    head_dim,
    stages,
    scale,
    x_ref,
    g_ref,
    key_ref,
    query_ref,
    raw_ref,
    codec_ref,
    finger_ref,
    fret_ref,
    table_ref,
    small_ref,
    decay_ref,
    skip_ref,
    mix_ref,
    gstep_ref,
    gkey_ref,
    gquery_ref,
    gcodec_ref,
    gsmall_ref,
    gfret_ref,
    gfinger_ref,
    gram_ref,
    ggram_ref,
    qextra_ref,
    kextra_ref,
    diag_ref,
    s_ref,
    p_ref,
    e_ref,
    b_ref,
    fo_ref,
    bo_ref,
    rows_ref,
    cols_ref,
    pre_ref,
    row_cross_ref,
    step_col_ref,
    cum_col_ref,
    tail_col_ref,
    meet_ref,
    skip_sum_ref,
    before_ref,
    key_t_ref,
    query_t_ref,
    all_ref,
    half_ref,
    got_half_ref,
    quarter_ref,
    got_ref,
    join_half_ref,
    join_ref,
    fsend,
    frecv,
    bsend,
    brecv,
    isend,
    irecv,
    ssend,
    srecv,
):
    me = lax.axis_index("seq")
    last = count - 1
    wide = 2 * head_dim
    heads = 2 * pairs
    length = key_ref.shape[0]
    barrier = pltpu.get_barrier_semaphore()

    def bit_of(axis, bit):
        return (lax.axis_index(axis) // bit) % 2

    def partner(axis, bit):
        return {axis: lax.axis_index(axis) + bit - 2 * bit * bit_of(axis, bit)}

    others = [stage for stage in stages if stage != ("seq", 1)]

    @pl.when(me > 0)
    def _():
        pl.semaphore_signal(barrier, inc=1, device_id={"seq": me - 1}, device_id_type=MESH)

    @pl.when(me < last)
    def _():
        pl.semaphore_signal(barrier, inc=1, device_id={"seq": me + 1}, device_id_type=MESH)

    for stage in others:
        pl.semaphore_signal(barrier, inc=1, device_id=partner(*stage), device_id_type=MESH)

    @pl.when(jnp.logical_and(me > 0, me < last))
    def _():
        pl.semaphore_wait(barrier, 2 + len(others))

    @pl.when(jnp.logical_or(me == 0, me == last))
    def _():
        pl.semaphore_wait(barrier, 1 + len(others))

    def icopy(at):
        return pltpu.make_async_remote_copy(
            src_ref=(finger_ref, fret_ref)[at],
            dst_ref=before_ref.at[at],
            send_sem=isend.at[at],
            recv_sem=irecv.at[at],
            device_id={"seq": me + 1},
            device_id_type=MESH,
        )

    @pl.when(me < last)
    def _():
        icopy(0).start()
        icopy(1).start()

    codec_hot = (
        lax.broadcasted_iota(jnp.int32, (table_ref.shape[1], length), 0) == codec_ref[...]
    ).astype(jnp.float32).astype(jnp.bfloat16)
    small_row = lax.broadcasted_iota(jnp.int32, (128, length), 0)
    fret_hot = (small_row == fret_ref[...]).astype(jnp.float32).astype(jnp.bfloat16)
    finger_hot = (
        (small_row == finger_ref[...] + FINGER_LANE).astype(jnp.float32).astype(jnp.bfloat16)
    )
    pre_step = (
        raw_ref[0] + exact(dot_nn, table_ref[...], codec_hot) + exact(dot_nn, small_ref[...], fret_hot)
    )
    pre_ref[...] = pre_step
    step = soft(pre_step)
    damping = exact(dot_nn, soft(small_ref[...]), finger_hot)
    head_row = lax.broadcasted_iota(jnp.int32, (heads, 1), 0)
    rate = jnp.zeros((heads, 1), jnp.float32)
    for h in range(heads):
        rate = jnp.where(head_row == h, decay_ref[h], rate)
    rate = jnp.exp(rate)
    key_t_ref[...] = key_ref[...].astype(jnp.float32).T.astype(jnp.bfloat16)
    query_t_ref[...] = query_ref[...].astype(jnp.float32).T.astype(jnp.bfloat16)
    place = lax.broadcasted_iota(jnp.int32, (length, length), 0)
    other = lax.broadcasted_iota(jnp.int32, (length, length), 1)

    @pl.when(me > 0)
    def _():
        pltpu.make_async_remote_copy(
            src_ref=finger_ref,
            dst_ref=before_ref.at[0],
            send_sem=isend.at[0],
            recv_sem=irecv.at[0],
            device_id={"seq": me - 1},
            device_id_type=MESH,
        ).wait_recv()
        pltpu.make_async_remote_copy(
            src_ref=fret_ref,
            dst_ref=before_ref.at[1],
            send_sem=isend.at[1],
            recv_sem=irecv.at[1],
            device_id={"seq": me - 1},
            device_id_type=MESH,
        ).wait_recv()

    @pl.when(me == 0)
    def _():
        before_ref[0] = finger_ref[...]
        before_ref[1] = fret_ref[...]

    spot = lax.broadcasted_iota(jnp.int32, (1, length), 1)

    def changed(ref, at):
        prior = jnp.where(spot == 0, pltpu.roll(before_ref[at], 1, 1), pltpu.roll(ref[...], 1, 1))
        return (ref[...] != prior).astype(jnp.float32)

    onset = jnp.maximum(changed(finger_ref, 0), changed(fret_ref, 1))
    onset = jnp.where(spot + me * length == 0, 0.0, onset)
    log_decay = -rate * step - onset * damping
    until = (place <= other).astype(jnp.float32).astype(jnp.bfloat16)
    cum = exact(dot_nn, log_decay, until)
    rise = jnp.exp(cum)
    tail_decay = jnp.exp(cum[:, length - 1 :] - cum)
    tail_weight = tail_decay * step
    for c in range(pairs):
        both = slice(2 * c, 2 * c + 2)
        rows_ref[c, 0:2, :] = cum[both]
        rows_ref[c, 2:4, :] = rise[both]
        rows_ref[c, 4:6, :] = tail_weight[both]
        rows_ref[c, 6:8, :] = step[both]
    def fcopy(c):
        return pltpu.make_async_remote_copy(
            src_ref=fo_ref.at[c],
            dst_ref=e_ref.at[c],
            send_sem=fsend.at[c],
            recv_sem=frecv.at[c],
            device_id={"seq": me + 1},
            device_id_type=MESH,
        )

    def bcopy(c):
        return pltpu.make_async_remote_copy(
            src_ref=bo_ref.at[c],
            dst_ref=b_ref.at[c],
            send_sem=bsend.at[c],
            recv_sem=brecv.at[c],
            device_id={"seq": me - 1},
            device_id_type=MESH,
        )

    gram_ref[...] = dot_nt(key_ref[...], query_ref[...])
    ggram_ref[...] = jnp.zeros_like(ggram_ref)
    qextra_ref[...] = jnp.zeros_like(qextra_ref)
    kextra_ref[...] = jnp.zeros_like(kextra_ref)
    step_col_ref[...] = jnp.zeros_like(step_col_ref)
    cum_col_ref[...] = jnp.zeros_like(cum_col_ref)
    tail_col_ref[...] = jnp.zeros_like(tail_col_ref)

    def lanes(c):
        return pl.ds(pl.multiple_of(c * wide, wide), wide)

    def halves(cols, at):
        side = lax.broadcasted_iota(jnp.int32, (length, wide), 1)
        return jnp.where(side < head_dim, cols[:, at : at + 1], cols[:, at + 1 : at + 2])

    def put(ref, head, col):
        side = lax.broadcasted_iota(jnp.int32, ref.shape, 1)
        ref[...] = jnp.where(side == head, col, ref[...])

    lane_side = lax.broadcasted_iota(jnp.int32, (1, wide), 1)

    def whole_decay(c):
        end = cols_ref[c, length - 1 : length, :]
        return jnp.where(lane_side < head_dim, end[:, 2:3], end[:, 3:4])

    def split(ref, c, line):
        ref[pl.ds(2 * c, 1), :] = jnp.where(lane_side < head_dim, line, 0.0)
        ref[pl.ds(2 * c + 1, 1), :] = jnp.where(lane_side < head_dim, 0.0, line)

    def own(c):
        cols_ref[c] = rows_ref[c].T
        cols = cols_ref[c]
        x = x_ref[:, lanes(c)].astype(jnp.float32)
        g = g_ref[:, lanes(c)].astype(jnp.float32)
        s_ref[c] = dot_nn(key_t_ref[...], (x * halves(cols, 4)).astype(jnp.bfloat16))
        p_ref[c] = dot_nn(query_t_ref[...], (g * halves(cols, 2)).astype(jnp.bfloat16))
        split(skip_sum_ref, c, jnp.sum(x * g, axis=0, keepdims=True))

    def inside(c):
        cols = cols_ref[c]
        x = x_ref[:, lanes(c)]
        g = g_ref[:, lanes(c)]
        mid = length // 2
        parts = []
        added = [None, None]
        for k in range(2):
            span = slice(k * head_dim, (k + 1) * head_dim)
            xh, gh = x[:, span], g[:, span]
            mixes, sums, rows = [], [], []
            for part in range(2):
                own_rows, start = slice(part * mid, (part + 1) * mid), part * mid
                gram = gram_ref[own_rows, start:]
                lower = lax.broadcasted_iota(jnp.int32, gram.shape, 0) <= lax.broadcasted_iota(
                    jnp.int32, gram.shape, 1
                )
                gap = rows_ref[c, k : k + 1, start:] - cols[own_rows, k : k + 1]
                decay = jnp.exp(jnp.where(lower, gap, -1e30))
                step = cols[own_rows, 6 + k : 7 + k]
                weights = ((gram * decay) * step).astype(jnp.bfloat16)
                mixes.append(dot_nn(weights, gh[start:]))
                masked = dot_nt(xh[own_rows], gh[start:]) * decay
                cross = masked * gram
                sums.append(jnp.sum(cross, axis=1, keepdims=True))
                rows.append(jnp.sum(cross * step, axis=0, keepdims=True))
                masked = masked * step
                added[part] = masked if added[part] is None else added[part] + masked
            parts.append(jnp.concatenate(mixes, axis=0))
            put(step_col_ref, 2 * c + k, jnp.concatenate(sums, axis=0))
            row_cross_ref[pl.ds(2 * c + k, 1), :] = jnp.concatenate(
                [rows[0][:, :mid], rows[0][:, mid:] + rows[1]], axis=1
            )
        ggram_ref[:mid, :] += added[0]
        ggram_ref[mid:, mid:] += added[1]
        gain = jnp.where(lane_side < head_dim, skip_ref[2 * c], skip_ref[2 * c + 1])
        diag_ref[:, lanes(c)] = jnp.concatenate(parts, axis=1) + gain * g.astype(jnp.float32)

    def forward(c):
        @pl.when(me > 0)
        def _():
            fcopy(c).wait_recv()

        @pl.when(me == 0)
        def _():
            e_ref[c] = jnp.zeros(e_ref.shape[1:], jnp.float32)

        @pl.when(me < last)
        def _():
            fo_ref[c] = whole_decay(c) * e_ref[c] + s_ref[c]
            fcopy(c).start()

    def backward(c):
        @pl.when(me < last)
        def _():
            bcopy(c).wait_recv()

        @pl.when(me == last)
        def _():
            b_ref[c] = jnp.zeros(b_ref.shape[1:], jnp.float32)

        @pl.when(me > 0)
        def _():
            bo_ref[c] = whole_decay(c) * b_ref[c] + p_ref[c]
            bcopy(c).start()

    def outside(c):
        cols = cols_ref[c]
        x = x_ref[:, lanes(c)]
        g = g_ref[:, lanes(c)]
        entering = e_ref[c]
        leaving = b_ref[c]
        state_low = entering.astype(jnp.bfloat16)
        grad_low = leaving.astype(jnp.bfloat16)
        split(meet_ref, c, jnp.sum(entering * leaving, axis=0, keepdims=True))
        pulled = dot_nn(key_ref[...], grad_low)
        mix_ref[:, lanes(c)] = (diag_ref[:, lanes(c)] + halves(cols, 4) * pulled).astype(jnp.bfloat16)
        key_wide = key_ref[...].astype(jnp.float32)
        query_wide = query_ref[...].astype(jnp.float32)
        qadd, kadd = None, None
        for k in range(2):
            span = slice(k * head_dim, (k + 1) * head_dim)
            read = dot_nt(g[:, span], state_low[:, span]) * cols[:, 2 + k : 3 + k]
            mixed = dot_nt(x[:, span], grad_low[:, span])
            tail = jnp.sum(mixed * key_wide, axis=1, keepdims=True)
            put(tail_col_ref, 2 * c + k, tail)
            put(cum_col_ref, 2 * c + k, jnp.sum(read * query_wide, axis=1, keepdims=True))
            mixed = mixed * cols[:, 4 + k : 5 + k]
            qadd = read if qadd is None else qadd + read
            kadd = mixed if kadd is None else kadd + mixed
        qextra_ref[...] += qadd
        kextra_ref[...] += kadd

    def within(c, work):
        @pl.when(jnp.logical_and(c >= 0, c < pairs))
        def _():
            work(c)

    def tick(t, carry):
        within(t, own)
        within(t - LAG * me, forward)
        within(t - LAG * (last - me), backward)
        within(t, inside)
        within(t - LAG * jnp.maximum(me, last - me), outside)
        return carry

    lax.fori_loop(0, pairs + LAG * last, tick, 0)
    low = ggram_ref[...].astype(jnp.bfloat16)
    gquery_ref[...] = (dot_tn(low, key_ref[...]) + qextra_ref[...]).astype(jnp.bfloat16)
    gkey_ref[...] = (dot_nn(low, query_ref[...]) + kextra_ref[...]).astype(jnp.bfloat16)

    @pl.when(me < last)
    def _():
        icopy(0).wait_send()
        icopy(1).wait_send()

    def drain(c, carry):
        @pl.when(me < last)
        def _():
            fcopy(c).wait_send()

        @pl.when(me > 0)
        def _():
            bcopy(c).wait_send()

        return carry

    lax.fori_loop(0, pairs, drain, 0)

    own_step = step_col_ref[...].T[:heads]
    grad_tail = tail_col_ref[...].T[:heads]
    tail_grad = grad_tail * tail_weight
    meet = jnp.sum(meet_ref[...], axis=1, keepdims=True)
    total_grad = jnp.sum(tail_grad, axis=1, keepdims=True) + rise[:, length - 1 :] * meet
    grad_cum = row_cross_ref[...] - step * own_step + cum_col_ref[...].T[:heads] - tail_grad
    grad_cum = jnp.where(spot == length - 1, grad_cum + total_grad, grad_cum)
    after = (place >= other).astype(jnp.float32).astype(jnp.bfloat16)
    grad_log = exact(dot_nn, grad_cum, after)
    grad_pre = (own_step + grad_tail * tail_decay - rate * grad_log) * logistic(pre_ref[...])
    gstep_ref[0] = grad_pre
    grad_codec = exact(dot_nt, grad_pre, codec_hot)
    grad_small = exact(dot_nt, grad_pre, fret_hot) + exact(
        dot_nt, -(onset * grad_log), finger_hot
    ) * logistic(small_ref[...])
    lane = lax.broadcasted_iota(jnp.int32, (1, 128), 1)
    grad_decay = -rate * jnp.sum(step * grad_log, axis=1, keepdims=True)
    grad_skip = jnp.sum(skip_sum_ref[...], axis=1, keepdims=True)
    grad_small = jnp.where(lane == DECAY_LANE, grad_decay, grad_small)
    grad_small = jnp.where(lane == SKIP_LANE, grad_skip, grad_small)
    tall, broad = heads // 8, table_ref.shape[1] // 128 + 1
    for a in range(tall):
        for b in range(broad):
            source = grad_small if b == broad - 1 else grad_codec
            at = 0 if b == broad - 1 else 128 * b
            all_ref[a * broad + b] = source[8 * a : 8 * a + 8, at : at + 128]
    for at in range(tall * broad, all_ref.shape[0]):
        all_ref[at] = jnp.zeros(all_ref.shape[1:], jnp.float32)

    def exchange(at, stage, src, dst):
        copy = pltpu.make_async_remote_copy(
            src_ref=src,
            dst_ref=dst,
            send_sem=ssend.at[at],
            recv_sem=srecv.at[at],
            device_id=partner(*stage),
            device_id_type=MESH,
        )
        copy.start()
        copy.wait()

    half, quarter = half_ref.shape[0], quarter_ref.shape[1]
    first, second = bit_of(*stages[0]), bit_of(*stages[1])
    exchange(0, stages[0], all_ref.at[pl.ds((1 - first) * half, half)], got_half_ref)
    half_ref[...] = all_ref[pl.ds(first * half, half)] + got_half_ref[...]
    exchange(1, stages[1], half_ref.at[pl.ds((1 - second) * quarter, quarter)], got_ref.at[0])
    quarter_ref[0] = half_ref[pl.ds(second * quarter, quarter)] + got_ref[0]
    rest = len(stages) - 2
    for at in range(rest):
        exchange(2 + at, stages[2 + at], quarter_ref.at[at], got_ref.at[at + 1])
        quarter_ref[at + 1] = quarter_ref[at] + got_ref[at + 1]
    mine = pl.ds(second * quarter, quarter)
    join_half_ref[mine] = quarter_ref[rest]
    exchange(2 + rest, stages[1], quarter_ref.at[rest], join_half_ref.at[mine])
    mine = pl.ds(first * half, half)
    join_ref[mine] = join_half_ref[...]
    exchange(3 + rest, stages[0], join_half_ref, join_ref.at[mine])
    for a in range(tall):
        for b in range(broad):
            value = join_ref[a * broad + b] * scale
            if b == broad - 1:
                rows = slice(8 * a, 8 * a + 8)
                gsmall_ref[rows, :] = value
                gfret_ref[rows, :] = value[:, : gfret_ref.shape[1]]
                gfinger_ref[rows, :] = value[:, FINGER_LANE : FINGER_LANE + gfinger_ref.shape[1]]
            else:
                gcodec_ref[8 * a : 8 * a + 8, 128 * b : 128 * b + 128] = value


def shards(
    mixer_in,
    step_raw,
    key_proj,
    query_proj,
    codec_ids,
    finger_ids,
    fret_ids,
    grad_out,
    decay_log,
    skip_gain,
    codec_bias,
    fret_bias,
    finger_damp,
):
    length, width = mixer_in.shape[1:]
    heads = decay_log.shape[0]
    head_dim = width // heads
    state = key_proj.shape[2]
    vocab = codec_bias.shape[1]
    frets, fingers = fret_bias.shape[1], finger_damp.shape[1]
    pairs = heads // 2
    wide = 2 * head_dim
    count = lax.axis_size("seq")
    stages = []
    for axis in ("dp", "seq"):
        bit = 1
        while bit < lax.axis_size(axis):
            stages.append((axis, bit))
            bit *= 2
    scale = float((lax.axis_size("dp") * count * length) ** (-0.5))
    small = jnp.pad(fret_bias, ((0, 0), (0, 128 - frets))) + jnp.pad(
        finger_damp, ((0, 0), (FINGER_LANE, 128 - FINGER_LANE - fingers))
    )
    tiles = (heads // 8) * (vocab // 128 + 1)
    tiles += -tiles % 4
    f32, bf16 = jnp.float32, jnp.bfloat16
    vmem = pl.BlockSpec(memory_space=pltpu.VMEM)
    smem = pl.BlockSpec(memory_space=pltpu.SMEM)
    states = pltpu.VMEM((pairs, state, wide), f32)
    column = pltpu.VMEM((length, 128), f32)
    sems = pltpu.SemaphoreType.DMA((pairs,))
    rounds = len(stages)
    grad_mixer, grad_step, grad_key, grad_query, grad_codec, grad_small, grad_fret, grad_finger = pl.pallas_call(
        functools.partial(mixer_kernel, count, pairs, head_dim, stages, scale),
        out_shape=[
            jax.ShapeDtypeStruct((length, width), bf16),
            jax.ShapeDtypeStruct((1, heads, length), f32),
            jax.ShapeDtypeStruct((length, state), bf16),
            jax.ShapeDtypeStruct((length, state), bf16),
            jax.ShapeDtypeStruct((heads, vocab), f32),
            jax.ShapeDtypeStruct((heads, 128), f32),
            jax.ShapeDtypeStruct((heads, frets), f32),
            jax.ShapeDtypeStruct((heads, fingers), f32),
        ],
        in_specs=[vmem] * 10 + [smem] * 2,
        out_specs=[vmem] * 8,
        scratch_shapes=[
            pltpu.VMEM((length, length), f32),
            pltpu.VMEM((length, length), f32),
            pltpu.VMEM((length, state), f32),
            pltpu.VMEM((length, state), f32),
            pltpu.VMEM((length, width), f32),
        ]
        + [states] * 6
        + [
            pltpu.VMEM((pairs, 8, length), f32),
            pltpu.VMEM((pairs, length, 8), f32),
            pltpu.VMEM((heads, length), f32),
            pltpu.VMEM((heads, length), f32),
            column,
            column,
            column,
            pltpu.VMEM((heads, wide), f32),
            pltpu.VMEM((heads, wide), f32),
            pltpu.VMEM((2, 1, length), jnp.int32),
            pltpu.VMEM((state, length), bf16),
            pltpu.VMEM((state, length), bf16),
            pltpu.VMEM((tiles, 8, 128), f32),
            pltpu.VMEM((tiles // 2, 8, 128), f32),
            pltpu.VMEM((tiles // 2, 8, 128), f32),
            pltpu.VMEM((rounds - 1, tiles // 4, 8, 128), f32),
            pltpu.VMEM((rounds - 1, tiles // 4, 8, 128), f32),
            pltpu.VMEM((tiles // 2, 8, 128), f32),
            pltpu.VMEM((tiles, 8, 128), f32),
        ]
        + [sems] * 4
        + [pltpu.SemaphoreType.DMA((2,))] * 2
        + [pltpu.SemaphoreType.DMA((rounds + 2,))] * 2,
        compiler_params=pltpu.CompilerParams(
            collective_id=0, has_side_effects=True, vmem_limit_bytes=56 * 1024 * 1024
        ),
    )(
        mixer_in[0],
        grad_out[0],
        key_proj[0],
        query_proj[0],
        step_raw,
        codec_ids,
        finger_ids,
        fret_ids,
        codec_bias,
        small,
        decay_log,
        skip_gain,
    )
    return (
        grad_mixer[None],
        grad_step,
        grad_key[None],
        grad_query[None],
        grad_small[:, DECAY_LANE],
        grad_small[:, SKIP_LANE],
        grad_codec,
        grad_fret,
        grad_finger,
    )


def solution(mesh):
    in_specs = (
        P("dp", "seq", None),
        P("dp", None, "seq"),
        P("dp", "seq", None),
        P("dp", "seq", None),
        P("dp", "seq"),
        P("dp", "seq"),
        P("dp", "seq"),
        P("dp", "seq", None),
        P(),
        P(),
        P(),
        P(),
        P(),
    )
    out_specs = (
        P("dp", "seq", None),
        P("dp", None, "seq"),
        P("dp", "seq", None),
        P("dp", "seq", None),
        P(),
        P(),
        P(),
        P(),
        P(),
    )
    return jax.shard_map(shards, mesh=mesh, in_specs=in_specs, out_specs=out_specs, check_vma=False)
```
